256 devices in a mesh: row: 16 (over x_hi, z), col: 16 (over x_lo, y, core).
Axes of the slice: x: 4 (x_hi: 2, x_lo: 2; x = x_hi * 2 + x_lo), y: 4, z: 8, core: 2. Of those that a mesh axis runs over, the one named last changes fastest.
Arguments:
- density: bfloat16 [32768, 1536], P(('row', 'col')), may hold values from -0.625 to 0.625
- pattern: int32 [256, 12], P(('row', 'col')), may hold values from 0 to 1, as said below
Outputs:
- band: bfloat16 [32768, 16, 2048], P('row', None, 'col')
The draws below stay inside these ranges and needn't reach their ends.
Inputs may be any that keep to these rules, and one draw needn't show every extreme that they name: `pattern`: each block row has its own share of stored blocks.
All inputs are finite; a program needn't handle non-finite values.
Results may differ from the reference program's by a relative error of at most 0.001.
Values may be sent and summed in bfloat16 or wider, within the bound.
No kernel may reach another device: no remote copies, remote signals or barrier semaphores. Data moves between devices by JAX's collectives and lax.ppermute only.
A program may use at most 64 MiB of HBM per device.

```python
import jax
import jax.numpy as jnp

BLOCK = 128
KB = 12
ROWS = 32768
STEPS = 16
N_ROW = 16
N_COL = 16


def draw_pattern(key, part):
    first_key, second_key = jax.random.split(jax.random.fold_in(key, 17))
    level = jax.random.randint(first_key, (ROWS // BLOCK, 1), 1, 9)
    ticket = jax.random.randint(second_key, (ROWS // BLOCK, KB), 0, 8)
    return (ticket < level).astype(jnp.int32)


def levels(stream_key, dims, pieces, smallest, top_value):
    def one(dim, shards_of):
        steps = jax.random.uniform(jax.random.fold_in(jax.random.fold_in(stream_key, 6), dim), (shards_of,), jnp.float32, smallest / len(pieces), top_value / len(pieces))
        return jnp.repeat(jnp.exp(steps), dims[dim] // shards_of).reshape((-1,) + (1,) * (len(dims) - dim - 1))

    loudness = one(*pieces[0])
    for cut in pieces[1:]:
        loudness = loudness * one(*cut)
    return loudness


def centred(key, dims, deviation, most, shards=(), kind=jnp.bfloat16):
    factor_of = levels(key, dims, shards, -0.22, 0.18) if shards else 1.0
    result = jax.random.normal(key, dims, jnp.float32) * deviation * factor_of
    return jnp.minimum(jnp.maximum(result, -most), most).astype(kind)


def setup_inputs(seed: int = 0) -> dict:
    key_of = jax.random.split(jax.random.key(seed), 3)
    return {
        "density": centred(key_of[0], (ROWS, KB * BLOCK), (KB * BLOCK // 16) ** -0.5, 0.625, ((0, 256),)),
        "pattern": draw_pattern(jax.random.fold_in(key_of[2], 71), 0),
    }


def reference(density, pattern):
    repeated = jnp.repeat(pattern, BLOCK, axis=0).astype(jnp.bfloat16)
    masked = (density.reshape(ROWS, KB, BLOCK) * repeated[:, :, None]).reshape(ROWS, KB * BLOCK)
    groups = masked.reshape(N_ROW, N_COL * BLOCK, KB * BLOCK).astype(jnp.float32)
    results = []
    for turn in range(STEPS):
        partner = jnp.roll(groups, -(N_ROW // 4 - turn), axis=0)
        product = jnp.einsum("rik,rjk->rij", groups, partner)
        results.append(product.astype(jnp.bfloat16).reshape(ROWS, N_COL * BLOCK))
    return jnp.stack(results, axis=1)
```

```python
import jax
import jax.numpy as jnp
from jax import lax
from jax.experimental import pallas as pl
from jax.experimental.pallas import tpu as pltpu
from jax.sharding import PartitionSpec as P

Y = 4
CORES = 2


def move(value, dx_hi=0, dz=0, dx_lo=0, dy=0, dcore=0):
    rows, cols = lax.axis_size("row"), lax.axis_size("col")
    deep = rows // 2
    pairs = []
    for r in range(rows):
        for c in range(cols):
            x_hi, z = divmod(r, deep)
            x_lo, rest = divmod(c, Y * CORES)
            y, core = divmod(rest, CORES)
            to_r = ((x_hi + dx_hi) % 2) * deep + (z + dz) % deep
            to_c = (((x_lo + dx_lo) % 2) * Y + (y + dy) % Y) * CORES + (core + dcore) % CORES
            pairs.append((r * cols + c, to_r * cols + to_c))
    return lax.ppermute(value, ("row", "col"), pairs)


def row_pieces(own):
    half = own.shape[0] // 2
    far = move(own, dx_hi=1)
    p1, m1 = move(own, dz=1), move(own, dz=-1)
    p2, m2 = move(p1, dz=1), move(m1, dz=-1)
    p3, m3 = move(p2, dz=1), move(m2, dz=-1)
    p4, m4 = move(p3[:half], dz=1), move(m3[half:], dz=-1)
    fp1, fm1 = move(far, dz=1), move(far, dz=-1)
    fp2, fm2 = move(p2, dx_hi=1), move(m2, dx_hi=1)
    fp3, fm3 = move(fp2, dz=1), move(fm2, dz=-1)
    fp4, fm4 = move(p4, dx_hi=1), move(m4, dx_hi=1)
    return [
        (own, 0, 0, 0), (far, 1, 0, 0),
        (p1, 0, -1, 0), (m1, 0, 1, 0), (p2, 0, -2, 0), (m2, 0, 2, 0), (p3, 0, -3, 0), (m3, 0, 3, 0),
        (p4, 0, -4, 0), (m4, 0, 4, half),
        (fp1, 1, -1, 0), (fm1, 1, 1, 0), (fp2, 1, -2, 0), (fm2, 1, 2, 0), (fp3, 1, -3, 0), (fm3, 1, 3, 0),
        (fp4, 1, -4, 0), (fm4, 1, 4, half),
    ]


def col_pieces(own):
    out = []
    for flip, v in ((0, own), (1, move(own, dx_lo=1))):
        out += [(v, flip, 0, 0), (move(v, dy=1), flip, -1, 0), (move(v, dy=-1), flip, 1, 0), (move(v, dy=2), flip, 2, 0)]
    return out + [(move(v, dcore=1), flip, y, 1) for v, flip, y, _ in out]


def product(left, right, offsets, block, width):
    deep = offsets // 2
    count = len(left)
    tall = 512
    rows = count * block
    per = tall // block

    def body(*refs):
        a_refs, b_refs = refs[:count], refs[count : count + len(right)]
        o_ref, a_buf, b_buf, stage, a_sem, b_sem = refs[count + len(right) :]
        step = pl.program_id(0)
        r, c = lax.axis_index("row"), lax.axis_index("col")

        @pl.when(step == 0)
        def _():
            x_hi, z = r // deep, lax.rem(r, deep)
            for ref, (_, flip, dz, first) in zip(b_refs, right):
                q = lax.rem(x_hi + flip, 2) * deep + lax.rem(z + dz + deep, deep)
                s = lax.rem(r + offsets // 4 - q + offsets, offsets)
                pltpu.make_async_copy(
                    ref, b_buf.at[s, pl.ds(first, ref.shape[0])], b_sem.at[s, 1 if first else 0]
                ).start()
            x_lo, y, core = c // (Y * CORES), lax.rem(c // CORES, Y), lax.rem(c, CORES)
            for ref, (_, flip, dy, other) in zip(a_refs, left):
                a = (lax.rem(x_lo + flip, 2) * Y + lax.rem(y + dy + Y, Y)) * CORES + lax.rem(core + other, CORES)
                pltpu.make_async_copy(ref, a_buf.at[a], a_sem.at[a]).start()
            for s in range(offsets):
                if s % deep == 0:
                    half = block // 2
                    pltpu.make_async_copy(b_refs[8], b_buf.at[s, pl.ds(0, half)], b_sem.at[s, 0]).wait()
                    pltpu.make_async_copy(b_refs[8], b_buf.at[s, pl.ds(half, half)], b_sem.at[s, 1]).wait()
                else:
                    pltpu.make_async_copy(b_refs[0], b_buf.at[s], b_sem.at[s, 0]).wait()

        for j in range(per):
            a = step * per + j
            pltpu.make_async_copy(a_refs[0], a_buf.at[a], a_sem.at[a]).wait()
        lhs = a_buf[pl.ds(step * per, per)].reshape(tall, width)
        for s in range(0, offsets, 2):
            rhs = b_buf[s : s + 2].reshape(2 * block, width)
            acc = lax.dot_general(lhs, rhs, (((1,), (1,)), ((), ())), preferred_element_type=jnp.float32)
            stage[pl.ds(s, tall, stride=offsets), :] = acc[:, :block]
            stage[pl.ds(s + 1, tall, stride=offsets), :] = acc[:, block:]
        o_ref[...] = stage[...].astype(o_ref.dtype)

    out = pl.pallas_call(
        body,
        grid=(rows // tall,),
        in_specs=[pl.BlockSpec(memory_space=pl.ANY)] * (count + len(right)),
        out_specs=pl.BlockSpec((tall * offsets, block), lambda i: (i, 0)),
        out_shape=jax.ShapeDtypeStruct((rows * offsets, block), jnp.bfloat16),
        scratch_shapes=[
            pltpu.VMEM((count, block, width), jnp.bfloat16),
            pltpu.VMEM((offsets, block, width), jnp.bfloat16),
            pltpu.VMEM((tall * offsets, block), jnp.float32),
            pltpu.SemaphoreType.DMA((count,)),
            pltpu.SemaphoreType.DMA((offsets, 2)),
        ],
        compiler_params=pltpu.CompilerParams(vmem_limit_bytes=32 << 20),
        name="band",
    )(*[v for v, *_ in left], *[v for v, *_ in right])
    return out.reshape(rows, offsets, block)


def local(density, pattern):
    block, width = density.shape
    present = pattern.reshape(1, width // block, 1).astype(jnp.bfloat16)
    own = (density.reshape(block, width // block, block) * present).reshape(block, width)
    right = row_pieces(own)
    left = col_pieces(own)
    return product(left, right, lax.axis_size("row"), block, width)


def solution(mesh):
    return jax.shard_map(
        local,
        mesh=mesh,
        in_specs=(P(("row", "col"), None), P(("row", "col"), None)),
        out_specs=P("row", None, "col"),
        check_vma=False,
    )
```
